32 devices in a mesh: blocks: 2 (over x), rows: 8 (over z, y), pairs: 2 (over core).
Axes of the slice: x: 2, y: 2, z: 4, core: 2. Of those that a mesh axis runs over, the one named last changes fastest.
Arguments:
- interferograms: bfloat16 [2, 1500, 256, 256], P(None, 'pairs', ('blocks', 'rows')), parts along dimension 2, may hold values from -6 to 6
- pair_dates: int32 [1500, 2], replicated, may hold values from 0 to 299, as said below
- mask_table: int32 [4, 1500], replicated, may hold values 0 or 1
- gap_dates: int32 [4, 30], replicated, may hold values from 0 to 299, as said below
- pattern_ids: int32 [256, 256], P(('blocks', 'rows')), parts along dimension 0, may hold values from 0 to 3
Outputs:
- corrected: float32 [256, 300, 256], P(('blocks', 'rows', 'pairs')), parts along dimension 0
The draws below stay inside these ranges and needn't reach their ends.
There are 2 independent parts, one for each index of `blocks`. The reference program is written for one: setup_inputs(seed, part) draws one part's arguments, and reference() takes and returns one part's arrays. A program takes and returns all parts, laid end to end along the dimension named above; an argument that names none is the same for every part. Nothing has to cross between parts.
Inputs may be any that keep to these rules, and one draw needn't show every extreme that they name: `pair_dates`: row k holds the earlier and the later date of pair k; the later exceeds the earlier by 1 to 5. `gap_dates`: each row lists 30 different dates. `pattern_ids`: each pixel belongs to one of 4 gap pattern classes.
All inputs are finite; a program needn't handle non-finite values.
Results may differ from the reference program's by a relative error of at most 0.0044.
Values may be sent and summed in bfloat16 or wider, within the bound.
No kernel may reach another device: no remote copies, remote signals or barrier semaphores. Data moves between devices by JAX's collectives and lax.ppermute only.
A program may use at most 192 MiB of HBM per device.

```python
import jax
import jax.numpy as jnp
from jax import lax

PAIRS = 1500
DATES = 300
NPAT = 4
GAPS = 30
SPAN = 5
RADIUS = 6
ROWS_DEV = 16
COLS = 256
HEIGHT = 128


def draw_pair_dates(key, part):
    key_early, key_span = jax.random.split(key)
    early = jax.random.randint(key_early, (PAIRS,), 0, DATES - 1)
    span = jax.random.randint(key_span, (PAIRS,), 1, SPAN + 1)
    late = jnp.minimum(early + span, DATES - 1)
    index = jnp.arange(PAIRS)
    early = jnp.where(index == 0, 0, early)
    late = jnp.where(index == 0, span, late)
    early = jnp.where(index == 1, DATES - 1 - span, early)
    late = jnp.where(index == 1, DATES - 1, late)
    return jnp.stack([early, late], axis=1).astype(jnp.int32)


def draw_gap_dates(key, part):
    keys = jax.random.split(jax.random.fold_in(key, 11), NPAT)
    shuffled = jax.vmap(lambda one_key: jax.random.permutation(one_key, DATES))(keys)[:, :GAPS]
    inner = jax.random.permutation(jax.random.fold_in(key, 7), DATES - 2)[:GAPS - 2] + 1
    first_row = jnp.concatenate([jnp.array([0, DATES - 1]), inner])
    return shuffled.at[0].set(first_row).astype(jnp.int32)


def set_ends(values, key, least, high):
    longest = values.shape.index(max(values.shape))
    spots = []
    for shift in (0, 1):
        where = [jax.random.randint(jax.random.fold_in(key, axis), (), 0, length) for axis, length in enumerate(values.shape)]
        where[longest] = (where[longest] + shift) % values.shape[longest]
        spots.append(tuple(where))
    return values.at[spots[0]].set(least).at[spots[1]].set(high)


def block_levels(own_key, extent, cuts, smallest, high):
    loudness = 1.0
    for dim, blocks in cuts:
        steps = jax.random.uniform(jax.random.fold_in(jax.random.fold_in(own_key, 6), dim), (blocks,), jnp.float32, smallest / len(cuts), high / len(cuts))
        loudness = loudness * jnp.repeat(jnp.exp(steps), extent[dim] // blocks).reshape((-1,) + (1,) * (len(extent) - 1 - dim))
    return loudness


def noise(own_key, dims, spread, most, pieces=(), held_as=jnp.bfloat16):
    values = spread * jax.random.normal(own_key, dims, jnp.float32)
    if pieces:
        values = values * block_levels(own_key, dims, pieces, -0.22, 0.18)
    return jnp.clip(values, -most, most).astype(held_as)


def setup_inputs(seed: int = 0, part: int = 0) -> dict:
    key_of = jax.random.split(jax.random.key(seed), 6)
    own_keys = jax.random.split(jax.random.fold_in(key_of[5], part), 6)
    interferograms = noise(own_keys[0], (2, PAIRS, HEIGHT, COLS), 1.0, 6.0, ((1, 2), (2, 8)))
    pair_dates = draw_pair_dates(jax.random.fold_in(key_of[5], 71), part)
    mask_table = set_ends((jax.random.randint(key_of[2], (NPAT, PAIRS), 0, 5) < 4).astype(jnp.int32), jax.random.fold_in(key_of[2], 1), 0, 1)
    gap_dates = draw_gap_dates(jax.random.fold_in(key_of[5], 71), part)
    pattern_ids = set_ends(jax.random.randint(own_keys[4], (HEIGHT, COLS), 0, NPAT), jax.random.fold_in(own_keys[4], 1), 0, NPAT - 1).astype(jnp.int32)
    return dict(interferograms=interferograms, pair_dates=pair_dates, mask_table=mask_table, gap_dates=gap_dates, pattern_ids=pattern_ids)


damping = 0.5
corr_length = 10.0
gauss_width = 2.0

def build_operators(pair_dates, mask_rows, gap_rows):
    dates = jnp.arange(DATES, dtype=jnp.int32)
    first_hot = (dates[None, :] == pair_dates[:, 0:1]).astype(jnp.float32)
    second_hot = (dates[None, :] == pair_dates[:, 1:2]).astype(jnp.float32)
    incidence = second_hot - first_hot
    gapped = jnp.any(gap_rows[:, :, None] == dates[None, None, :], axis=1).astype(jnp.float32)
    lag = jnp.abs(dates[:, None] - dates[None, :]).astype(jnp.float32)
    cov = jnp.exp(-lag / corr_length)
    ident = jnp.eye(DATES, dtype=jnp.float32)
    hp = lax.Precision.HIGHEST

    def single(args):
        valid_row, gap_row = args
        gap_first = jnp.dot(first_hot, gap_row, precision=hp)
        gap_second = jnp.dot(second_hot, gap_row, precision=hp)
        keep = valid_row.astype(jnp.float32) * (1.0 - gap_first) * (1.0 - gap_second)
        weighted = incidence * keep[:, None]
        normal = jnp.dot(weighted.T, incidence, precision=hp) + damping * ident
        factor = jnp.linalg.cholesky(normal)
        solved = jax.scipy.linalg.cho_solve((factor, True), weighted.T)
        observed = 1.0 - gap_row
        masked = cov * observed[:, None] * observed[None, :] + jnp.diag(gap_row)
        cross = cov * observed[:, None] * gap_row[None, :]
        factor_two = jnp.linalg.cholesky(masked)
        weights = jax.scipy.linalg.cho_solve((factor_two, True), cross)
        return solved + jnp.dot(weights.T, solved, precision=hp)
    return lax.map(single, (mask_rows, gapped)).astype(jnp.bfloat16)

def multilook_one(pair_planes):
    height = pair_planes.shape[1]
    width = pair_planes.shape[2]
    planes = pair_planes.astype(jnp.float32)
    padded = jnp.pad(planes, ((0, 0), (2, 2), (2, 2)))
    along = sum((padded[:, offset:offset + height, :] for offset in range(5)))
    boxed = sum((along[:, :, offset:offset + width] for offset in range(5)))
    modulus = jnp.sqrt(boxed[0] * boxed[0] + boxed[1] * boxed[1])
    return (boxed[1] / jnp.maximum(modulus, 1.0)).astype(jnp.bfloat16)

def gauss_kernel():
    spots = jnp.arange(-RADIUS, RADIUS + 1, dtype=jnp.float32)
    raw = jnp.exp(-spots * spots / (2.0 * gauss_width * gauss_width))
    return raw / jnp.sum(raw)

def select_class(by_class, classes_here):
    labels = jnp.arange(by_class.shape[1], dtype=jnp.int32)
    hit = classes_here[:, None, None, :] == labels[None, :, None, None]
    return lax.optimization_barrier(jnp.sum(jnp.where(hit, by_class, 0.0), axis=1))

def reference(interferograms, pair_dates, mask_table, gap_dates, pattern_ids):
    height = interferograms.shape[2]
    width = interferograms.shape[3]
    looks = lax.map(multilook_one, jnp.moveaxis(interferograms, 1, 0))
    operators = build_operators(pair_dates, mask_table, gap_dates).astype(jnp.float32)
    block_rows = ROWS_DEV // 2

    def invert(start):
        piece = lax.dynamic_slice_in_dim(looks, start, block_rows, 1).astype(jnp.float32)
        classes_here = lax.dynamic_slice_in_dim(pattern_ids, start, block_rows, 0)
        by_class = jnp.einsum('qtk,krc->rqtc', operators, piece, precision=lax.Precision.HIGHEST)
        return select_class(by_class, classes_here)
    starts = jnp.arange(height // block_rows, dtype=jnp.int32) * block_rows
    series = lax.map(invert, starts).reshape(height, DATES, width)
    kernel = gauss_kernel()
    padded = jnp.pad(series, ((RADIUS, RADIUS), (0, 0), (RADIUS, RADIUS)))
    along = sum((kernel[offset] * padded[offset:offset + height] for offset in range(2 * RADIUS + 1)))
    screen = sum((kernel[offset] * along[:, :, offset:offset + width] for offset in range(2 * RADIUS + 1)))
    return series - screen
```

```python
import functools

import jax
import jax.numpy as jnp
import numpy as np
from jax import lax
from jax.experimental import pallas as pl
from jax.experimental.pallas import tpu as pltpu
from jax.sharding import PartitionSpec as P

f32 = jnp.float32
bf16 = jnp.bfloat16
DATES = 300
RADIUS = 6
REACH = 2
SPAN = 5
DAMP = 0.5
CORR = 10.0
WIDTH = 2.0
NCHUNK = 3
KB = 64
VMEM_LIMIT = 60 * 2**20


def ops_kernel(nq, T, Tp, Tl, early_ref, late_ref, mask_ref, gap_ref, out_ref,
               band, lfac, dinv, ymat):
    Kp = early_ref.shape[1]
    early = early_ref[...]
    late = late_ref[...]
    tt = lax.broadcasted_iota(jnp.int32, (Tp, Kp), 0)
    eh = (tt == early).astype(f32)
    lh = (tt == late).astype(f32)
    ehb = eh.astype(bf16); lhb = lh.astype(bf16)
    gap = gap_ref[...]
    gapb = gap.astype(bf16)
    ge = jnp.dot(gapb, ehb, preferred_element_type=f32)
    gl = jnp.dot(gapb, lhb, preferred_element_type=f32)
    keep = mask_ref[...].astype(f32) * (1.0 - ge) * (1.0 - gl)
    span = late - early
    stack = jnp.concatenate([jnp.where(span == d, keep, 0.0) for d in range(1, SPAN + 1)], axis=0).astype(bf16)
    nt = (((1,), (1,)), ((), ()))
    cnt = lax.dot_general(ehb, stack, nt, preferred_element_type=f32)
    deg = lax.dot_general((eh + lh).astype(bf16), keep.astype(bf16), nt, preferred_element_type=f32) + DAMP
    for q in range(8):
        band[0, pl.ds(q, Tp, stride=8), :] = jnp.broadcast_to(deg[:, q:q + 1], (Tp, 128))
        for d in range(1, SPAN + 1):
            c = (d - 1) * 8 + q
            band[d, pl.ds(q, Tp, stride=8), :] = jnp.broadcast_to(-cnt[:, c:c + 1], (Tp, 128))
    band[:, Tp * 8:, :] = jnp.ones(band[:, Tp * 8:, :].shape, f32)
    nl = Tl // 128
    lane = [lax.broadcasted_iota(jnp.int32, (8, 128), 1) + 128 * c for c in range(nl)]
    def brow(d, t):
        return band[d, pl.ds(pl.multiple_of(t * 8, 8), 8), :]
    def unit(t):
        return [(lane[c] == t).astype(f32) for c in range(nl)]
    n = SPAN + 1
    w0 = tuple(tuple(brow(i - k, k) for k in range(i + 1)) for i in range(n))
    y0 = tuple(tuple(unit(i)) for i in range(n))
    def fwd(j, carry):
        w, y = carry
        r = 1.0 / w[0][0]
        l = [None] + [w[i][0] * r for i in range(1, n)]
        base = pl.multiple_of(j * 8, 8)
        dinv[pl.ds(base, 8), :] = r
        for i in range(1, n):
            lfac[i - 1, pl.ds(base, 8), :] = l[i]
        for c in range(nl):
            ymat[c, pl.ds(base, 8), :] = y[0][c] * r
        nw = [tuple(w[i][k] - l[i] * w[k][0] for k in range(1, i + 1)) for i in range(1, n)]
        nw.append(tuple(brow(SPAN - k, j + 1 + k) for k in range(n)))
        ny = [tuple(y[i][c] - l[i] * y[0][c] for c in range(nl)) for i in range(1, n)]
        ny.append(tuple(unit(j + n)))
        return tuple(nw), tuple(ny)
    lax.fori_loop(0, T, fwd, (w0, y0))
    ymat[:, T * 8:, :] = jnp.zeros(ymat[:, T * 8:, :].shape, f32)
    zero = ymat[0, T * 8:T * 8 + 8, :]
    def back(s, x):
        j = T - 1 - s
        base = pl.multiple_of(j * 8, 8)
        l = [lfac[i, pl.ds(base, 8), :] for i in range(SPAN)]
        new = []
        for c in range(nl):
            v = ymat[c, pl.ds(base, 8), :]
            for i in reversed(range(SPAN)):
                v = v - l[i] * x[i][c]
            ymat[c, pl.ds(base, 8), :] = v
            new.append(v)
        return (tuple(new),) + x[:-1]
    lax.fori_loop(0, T, back, tuple(tuple(zero for _ in range(nl)) for _ in range(SPAN)))
    gapt = gap.T
    ss = lax.broadcasted_iota(jnp.int32, (Tp, Tp), 1)
    gg = lax.broadcasted_iota(jnp.int32, (Tp, Tp), 0)
    inc = lh - eh
    gcol = lax.broadcasted_iota(jnp.int32, (Tp, 1), 0).astype(f32)
    sf = ss.astype(f32)
    for q in range(nq):
        obs = (gap[q:q + 1, :] == 0.0) & (ss < T)
        left = jnp.max(jnp.where(obs & (ss < gg), sf, -1.0), axis=1, keepdims=True)
        right = jnp.min(jnp.where(obs & (ss > gg), sf, 1e9), axis=1, keepdims=True)
        isgap = gapt[:, q:q + 1]
        a = jnp.where(left >= 0.0, jnp.exp(-(gcol - left) / CORR), 0.0)
        b = jnp.where(right < 1e8, jnp.exp(-(right - gcol) / CORR), 0.0)
        den = isgap / (1.0 - a * a * b * b)
        wl = a * (1.0 - b * b) * den
        wr = b * (1.0 - a * a) * den
        krig = jnp.where(sf == left, wl, 0.0) + jnp.where(sf == right, wr, 0.0)
        krig = krig + (ss == gg).astype(f32)
        inv = jnp.concatenate([ymat[c, pl.ds(q, Tp, stride=8), :] for c in range(nl)], axis=1)
        full = jnp.dot(krig, inv, precision=lax.Precision.HIGHEST, preferred_element_type=f32)
        full = full[:, :Tp]
        h = full.astype(bf16); rem = full - h.astype(f32)
        m = rem.astype(bf16); lo = (rem - m.astype(f32)).astype(bf16)
        wq = (inc * keep[q:q + 1, :]).astype(bf16)
        res = jnp.dot(h, wq, preferred_element_type=f32) + (
            jnp.dot(m, wq, preferred_element_type=f32) + jnp.dot(lo, wq, preferred_element_type=f32))
        out_ref[q * Tp:(q + 1) * Tp, :] = res.astype(bf16)

def build_ops(early, late, mask, gapped, T):
    Kp = early.shape[1]; Tp = gapped.shape[1]; nq = 4; Tl = -(-Tp // 128) * 128
    rows = (Tp + 8) * 8
    return pl.pallas_call(
        functools.partial(ops_kernel, nq, T, Tp, Tl),
        out_shape=jax.ShapeDtypeStruct((nq * Tp, Kp), bf16),
        in_specs=[pl.BlockSpec(memory_space=pltpu.VMEM)] * 4,
        out_specs=pl.BlockSpec(memory_space=pltpu.VMEM),
        scratch_shapes=[pltpu.VMEM((SPAN + 1, rows, 128), f32), pltpu.VMEM((SPAN, Tp * 8, 128), f32),
                        pltpu.VMEM((Tp * 8, 128), f32), pltpu.VMEM((Tl // 128, Tp * 8, 128), f32)],
        compiler_params=pltpu.CompilerParams(vmem_limit_bytes=VMEM_LIMIT),
        name="operators",
    )(early, late, mask, gapped)


def band_matrix(columns):
    at = np.arange(columns)
    return jnp.asarray(np.abs(at[:, None] - at[None, :]) <= REACH, dtype=bf16)


def gauss_taps():
    spots = np.arange(-RADIUS, RADIUS + 1, dtype=np.float64)
    raw = np.exp(-spots * spots / (2.0 * WIDTH * WIDTH))
    return raw / raw.sum()


def gauss_matrices(columns):
    taps = gauss_taps()
    at = np.arange(columns)
    gap = at[None, :] - at[:, None]
    full = np.where(np.abs(gap) <= RADIUS, taps[np.clip(gap + RADIUS, 0, 2 * RADIUS)], 0.0)
    full = jnp.asarray(full, dtype=f32)
    high = full.astype(bf16)
    low = (full - high.astype(f32)).astype(bf16)
    return jnp.stack([high, low])


def call(kernel, **kw):
    limit = pltpu.CompilerParams(vmem_limit_bytes=VMEM_LIMIT)
    return pl.pallas_call(kernel, compiler_params=limit, **kw)


def looks_of(real, imag):
    power = jnp.maximum(real * real + imag * imag, 1.0)
    return imag * lax.rsqrt(power)


def edge_kernel(strip, side_ref, x_ref, own_ref, own_in_ref, sib_ref, sib_in_ref, wide):
    side = side_ref[0]
    kb = x_ref.shape[1]
    for plane in range(2):
        whole = x_ref[plane].astype(f32).reshape(kb * strip, x_ref.shape[3])
        for h in range(wide.shape[1]):
            wide[plane, h] = whole[:, h * 128:(h + 1) * 128]
    for plane in range(2):
        for h in range(wide.shape[1]):
            for i in range(4):
                own_row = i + side * (strip - 1 - 2 * i)
                sib_row = strip - 1 - own_row
                lanes = slice(h * 128, (h + 1) * 128)
                mine = wide[plane, h, pl.ds(own_row, kb, stride=strip), :].astype(bf16)
                theirs = wide[plane, h, pl.ds(sib_row, kb, stride=strip), :].astype(bf16)
                (own_ref if i < 2 else own_in_ref)[plane, i % 2, :, lanes] = mine
                (sib_ref if i < 2 else sib_in_ref)[plane, i % 2, :, lanes] = theirs


def edges(side, x, chunk, size):
    planes, pairs, strip, columns = x.shape
    steps = size // KB
    out = jax.ShapeDtypeStruct((planes, 2, size, columns), bf16)
    return call(
        functools.partial(edge_kernel, strip),
        out_shape=[out] * 4,
        grid_spec=pltpu.PrefetchScalarGridSpec(
            num_scalar_prefetch=1,
            grid=(steps,),
            in_specs=[pl.BlockSpec((planes, KB, strip, columns), lambda g, s: (0, chunk * steps + g, 0, 0))],
            out_specs=[pl.BlockSpec((planes, 2, KB, columns), lambda g, s: (0, 0, g, 0))] * 4,
            scratch_shapes=[pltpu.VMEM((planes, columns // 128, KB * strip, 128), f32)],
        ),
        name="edges",
    )(side, x)


def inner_kernel(strip, pairs, side_ref, x_ref, band_ref, mine_ref, send_ref, wide, held):
    side = side_ref[0]
    kb = x_ref.shape[1]
    half = strip // 2
    base = pl.program_id(0) * kb
    for plane in range(2):
        summed = jnp.dot(x_ref[plane].reshape(kb * strip, x_ref.shape[3]), band_ref[...],
                         preferred_element_type=f32)
        for h in range(wide.shape[1]):
            wide[plane, h] = summed[:, h * 128:(h + 1) * 128]

    def part(s, carry):
        start = pl.multiple_of(s * 16, 16)
        valid = lax.broadcasted_iota(jnp.int32, (16, 128), 0) + (base + start) < pairs
        for h in range(wide.shape[1]):
            rows = [[wide[plane, h, pl.ds(start * strip + y, 16, stride=strip), :] for y in range(strip)]
                    for plane in range(2)]
            twos = [[rows[plane][y] + rows[plane][y + 1] for y in range(strip - 1)] for plane in range(2)]
            for y in range(REACH, strip - REACH):
                real, imag = [twos[plane][y - 2] + twos[plane][y] + rows[plane][y + 2] for plane in range(2)]
                value = jnp.where(valid, looks_of(real, imag), 0.0).astype(bf16)
                low = y < half
                which = side if low else 1 - side
                at = y - REACH if low else strip - 1 - REACH - y
                held[which, at, pl.ds(start, 16), h * 128:(h + 1) * 128] = value
        return carry

    lax.fori_loop(0, kb // 16, part, 0)
    mine_ref[...] = held[0]
    send_ref[...] = held[1]


def inner_looks(side, x, band, padded):
    planes, pairs, strip, columns = x.shape
    rows = strip // 2 - REACH
    out = jax.ShapeDtypeStruct((rows, padded, columns), bf16)
    return call(
        functools.partial(inner_kernel, strip, pairs),
        out_shape=[out] * 2,
        grid_spec=pltpu.PrefetchScalarGridSpec(
            num_scalar_prefetch=1,
            grid=(padded // KB,),
            in_specs=[pl.BlockSpec((planes, KB, strip, columns), lambda g, s: (0, g, 0, 0)),
                      pl.BlockSpec((columns, columns), lambda g, s: (0, 0))],
            out_specs=[pl.BlockSpec((rows, KB, columns), lambda g, s: (0, g, 0))] * 2,
            scratch_shapes=[pltpu.VMEM((planes, columns // 128, KB * strip, 128), f32),
                            pltpu.VMEM((2, rows, KB, columns), bf16)],
        ),
        name="inner_looks",
    )(side, x, band)


def edge_looks_kernel(pairs, offset, *refs):
    band = refs[6][...]
    base = pl.program_id(0) * refs[0].shape[2] + offset
    for group, out_ref in ((refs[0:3], refs[7]), (refs[3:6], refs[8])):
        kb = out_ref.shape[1]
        rows = []
        for ref in group:
            flat = ref[...].reshape(4 * kb, ref.shape[3])
            summed = jnp.dot(flat, band, preferred_element_type=f32)
            rows.append(summed.reshape(2, 2, kb, ref.shape[3]))
        near, inner, outer = rows
        valid = lax.broadcasted_iota(jnp.int32, (kb, band.shape[1]), 0) + base < pairs
        first = [(outer[p, 1] + outer[p, 0]) + (near[p, 0] + near[p, 1]) + inner[p, 0] for p in range(2)]
        second = [(outer[p, 0] + near[p, 0]) + (near[p, 1] + inner[p, 0]) + inner[p, 1] for p in range(2)]
        out_ref[0] = jnp.where(valid, looks_of(*first), 0.0).astype(bf16)
        out_ref[1] = jnp.where(valid, looks_of(*second), 0.0).astype(bf16)


def edge_looks(parts, band, pairs, offset):
    planes, _, size, columns = parts[0].shape
    out = jax.ShapeDtypeStruct((2, size, columns), bf16)
    return call(
        functools.partial(edge_looks_kernel, pairs, offset),
        out_shape=[out] * 2,
        grid=(size // KB,),
        in_specs=[pl.BlockSpec((planes, 2, KB, columns), lambda g: (0, 0, g, 0))] * 6
        + [pl.BlockSpec((columns, columns), lambda g: (0, 0))],
        out_specs=[pl.BlockSpec((2, KB, columns), lambda g: (0, g, 0))] * 2,
        name="edge_looks",
    )(*parts, band)


def class_series(op_ref, looks, ids, depth):
    chosen = None
    classes = op_ref.shape[0] // depth
    for q in range(classes):
        total = None
        for column, piece in looks:
            part = jnp.dot(op_ref[q * depth:(q + 1) * depth, column:column + piece.shape[0]], piece,
                           preferred_element_type=f32)
            total = part if total is None else total + part
        chosen = total if chosen is None else jnp.where(ids == q, total, chosen)
    return jnp.where((ids >= 0) & (ids < classes), chosen, 0.0)


def invert_kernel(strip, depth, first, side_ref, op_ref, ids_ref, mine_ref, theirs_ref, out_ref, send_ref):
    i = pl.program_id(0) + first
    row = i + side_ref[0] * (strip - 1 - 2 * i)
    ids = ids_ref[pl.ds(row, 1), :]
    looks = [(0, mine_ref[0]), (mine_ref.shape[1], theirs_ref[0])]
    series = class_series(op_ref, looks, ids, depth)
    out_ref[0] = series
    send_ref[0] = series.astype(bf16)


def invert(side, operators, ids, mine, theirs, depth):
    rows, padded, columns = mine.shape
    strip = ids.shape[0]
    whole = lambda a: pl.BlockSpec(a.shape, lambda g, s: (0,) * a.ndim)
    out = [jax.ShapeDtypeStruct((rows, depth, columns), t) for t in (f32, bf16)]
    return call(
        functools.partial(invert_kernel, strip, depth, REACH),
        out_shape=out,
        grid_spec=pltpu.PrefetchScalarGridSpec(
            num_scalar_prefetch=1,
            grid=(rows,),
            in_specs=[whole(operators), whole(ids)]
            + [pl.BlockSpec((1, padded, columns), lambda g, s: (g, 0, 0))] * 2,
            out_specs=[pl.BlockSpec((1, depth, columns), lambda g, s: (g, 0, 0))] * 2,
        ),
        name="invert",
    )(side, operators, ids, mine, theirs)


def invert_edge_kernel(strip, depth, padded, side_ref, op_ref, ids_ref, *refs):
    count = (len(refs) - 2) // 2
    out_ref, send_ref = refs[-2:]
    size = refs[0].shape[1]
    for i in range(2):
        row = i + side_ref[0] * (strip - 1 - 2 * i)
        ids = ids_ref[pl.ds(row, 1), :]
        looks = [(c * size, refs[c][i]) for c in range(count)]
        looks += [(padded + c * size, refs[count + c][i]) for c in range(count)]
        series = class_series(op_ref, looks, ids, depth)
        out_ref[i] = series
        send_ref[i] = series.astype(bf16)


def invert_edge(side, operators, ids, mine, theirs, depth, padded):
    columns = ids.shape[1]
    out = [jax.ShapeDtypeStruct((2, depth, columns), t) for t in (f32, bf16)]
    return call(
        functools.partial(invert_edge_kernel, ids.shape[0], depth, padded),
        out_shape=out,
        in_specs=[pl.BlockSpec(memory_space=pltpu.SMEM)]
        + [pl.BlockSpec(memory_space=pltpu.VMEM)] * (2 + len(mine) + len(theirs)),
        out_specs=[pl.BlockSpec(memory_space=pltpu.VMEM)] * 2,
        name="invert_edge",
    )(side, operators, ids, *mine, *theirs)


def screen_kernel(side_ref, gauss_ref, late_ref, mid_ref, sib_ref, near_ref, far_ref, out_ref):
    taps = [float(t) for t in gauss_taps()]
    own = [late_ref[i] for i in range(2)] + [mid_ref[i] for i in range(mid_ref.shape[0])]
    count = len(own)
    side = side_ref[0]
    depth, columns = own[0].shape

    def row(i):
        if i >= count:
            return sib_ref[2 * count - 1 - i - 2].astype(f32)
        if i >= 0:
            return own[i]
        return (near_ref[-1 - i] if i >= -2 else far_ref[-3 - i]).astype(f32)

    rows = {i: row(i) for i in range(-RADIUS, count + RADIUS)}
    smooth = []
    for i in range(count):
        total = taps[RADIUS] * rows[i]
        for a in range(1, RADIUS + 1):
            total = total + taps[RADIUS + a] * (rows[i - a] + rows[i + a])
        smooth.append(total)
    high, low = gauss_ref[0], gauss_ref[1]
    for i in range(count):
        upper = smooth[i].astype(bf16)
        lower = (smooth[i] - upper.astype(f32)).astype(bf16)
        screen = jnp.dot(upper, high, preferred_element_type=f32) + (
            jnp.dot(upper, low, preferred_element_type=f32) + jnp.dot(lower, high, preferred_element_type=f32))
        at = i + side * (count - 1 - 2 * i)
        out_ref[pl.ds(at, 1)] = (own[i] - screen)[None]


def screened(side, gauss, late, mid, sib, near, far, dates):
    columns = late.shape[2]
    count = late.shape[0] + mid.shape[0]
    block = 16
    piece = lambda a: pl.BlockSpec((a.shape[0], block, columns), lambda g, s: (0, g, 0))
    return call(
        screen_kernel,
        out_shape=jax.ShapeDtypeStruct((count, dates, columns), f32),
        grid_spec=pltpu.PrefetchScalarGridSpec(
            num_scalar_prefetch=1,
            grid=(pl.cdiv(dates, block),),
            in_specs=[pl.BlockSpec(gauss.shape, lambda g, s: (0, 0, 0))]
            + [piece(a) for a in (late, mid, sib, near, far)],
            out_specs=pl.BlockSpec((count, block, columns), lambda g, s: (0, g, 0)),
        ),
        name="screen",
    )(side, gauss, late, mid, sib, near, far)


def pair_tables(side, pair_dates, mask_table, gap_dates, half, padded, depth):
    def split(rows):
        rows = rows.reshape(rows.shape[0], 2, half)
        rows = jnp.where(side[0] == 0, rows, rows[:, ::-1])
        return rows

    table = jnp.concatenate([pair_dates.T + 1, mask_table], axis=0)
    table = jnp.pad(split(table), ((0, 0), (0, 0), (0, padded - half))).reshape(-1, 2 * padded)
    early, late = table[0:1] - 1, table[1:2] - 1
    mask = jnp.pad(table[2:], ((0, 8 - mask_table.shape[0]), (0, 0)))
    spots = jnp.arange(depth, dtype=jnp.int32)
    gapped = jnp.any(gap_dates[:, :, None] == spots[None, None, :], axis=1).astype(f32)
    return early, late, mask, jnp.pad(gapped, ((0, 8 - gapped.shape[0]), (0, 0)))


def body(x, pair_dates, mask_table, gap_dates, pattern_ids):
    planes, half, strip, columns = x.shape
    depth = -(-DATES // 16) * 16
    size = -(-half // (NCHUNK * KB)) * KB
    padded = NCHUNK * size
    side = lax.axis_index("pairs").astype(jnp.int32).reshape(1)
    band = band_matrix(columns)
    count = lax.axis_size("rows")
    facing, crossing = [], []
    for r in range(count - 1):
        low, high = 2 * r, 2 * r + 2
        facing += [(low + 1, high), (high, low + 1)]
        crossing += [(low, high), (high + 1, low + 1)]
    both = [(0, 1), (1, 0)]
    hop = lambda v, table: lax.ppermute(v, ("rows", "pairs"), table)
    swap = lambda v: lax.ppermute(v, "pairs", both)

    parts = []
    for c in range(NCHUNK):
        own, own_in, sib, sib_in = edges(side, x, c, size)
        outer_other = hop(own, facing)
        outer_own = hop(sib, crossing)
        parts.append((own, own_in, outer_own, swap(sib), swap(sib_in), outer_other))

    mine, send = inner_looks(side, x, band, padded)
    theirs = swap(send)
    tables = pair_tables(side, pair_dates, mask_table, gap_dates, half, padded, depth)
    operators = build_ops(*tables, DATES)
    mid, mid_send = invert(side, operators, pattern_ids, mine, theirs, depth)
    sib_rows = swap(mid_send)
    far = hop(mid_send[:4], facing)

    pieces = [edge_looks(p, band, half, c * size) for c, p in enumerate(parts)]
    late, late_send = invert_edge(side, operators, pattern_ids, [p[0] for p in pieces], [p[1] for p in pieces],
                                  depth, padded)
    near = hop(late_send, facing)
    return screened(side, gauss_matrices(columns), late, mid, sib_rows, near, far, DATES)


def solution(mesh):
    placed = (
        P(None, "pairs", ("blocks", "rows"), None),
        P(),
        P(),
        P(),
        P(("blocks", "rows"), None),
    )
    return jax.shard_map(
        body,
        mesh=mesh,
        in_specs=placed,
        out_specs=P(("blocks", "rows", "pairs"), None, None),
        check_vma=False,
    )
```
